32 devices in a mesh: tm: 16 (over z, x, core), space: 2 (over y).
Axes of the slice: x: 2, y: 2, z: 4, core: 2. Of those that a mesh axis runs over, the one named last changes fastest.
Arguments:
- stream: bfloat16 [32, 12, 40, 2240], P('tm', 'space'), may hold values from -6 to 6
- queries: bfloat16 [32, 12, 40, 2240], P('tm', 'space'), may hold values from -6 to 6
- keys: bfloat16 [32, 12, 40, 2240], P('tm', 'space'), may hold values from -6 to 6
- values: bfloat16 [32, 12, 40, 2240], P('tm', 'space'), may hold values from -6 to 6
- state_in: float32 [20, 112, 112], replicated, may hold values from -120 to 120
- keysum_in: float32 [20, 112], replicated, may hold values from 100 to 1000
- attn_gate: float32 [2240], replicated, may hold values from 2 to 20
- ffn_shift: float32 [2240], replicated, may hold values from -3 to 3
- ffn_scale: float32 [2240], replicated, may hold values from -3 to 3
- w_up: bfloat16 [2240, 5600], P('tm'), may hold values from -0.125 to 0.125
- conv_weight: float32 [3, 3, 5600], replicated, may hold values from -2 to 2
- conv_bias: float32 [5600], replicated, may hold values from -3 to 3
Outputs:
- mixed: bfloat16 [32, 12, 40, 2240], P('tm', 'space')
- hidden: bfloat16 [32, 12, 40, 2800], P('tm', 'space')
The draws below stay inside these ranges and needn't reach their ends.
All inputs are finite; a program needn't handle non-finite values.
Results may differ from the reference program's by a relative error of at most 0.0076.
Values may be sent and summed in bfloat16 or wider, within the bound.
No kernel may reach another device: no remote copies, remote signals or barrier semaphores. Data moves between devices by JAX's collectives and lax.ppermute only.
A program may use at most 192 MiB of HBM per device.

```python
import math
import jax
import jax.numpy as jnp
from jax import lax

HEADS = 20
HEAD_DIM = 112
D = 2240
FW = 2800
COLS = 40
FRAMES = 32
ROWS = 12


def level_of(rng, shape, split, low, high):
    def one(axis_at, parts):
        heights = jax.random.uniform(jax.random.fold_in(jax.random.fold_in(rng, 6), axis_at), (parts,), jnp.float32, low / len(split), high / len(split))
        return jnp.repeat(jnp.exp(heights), shape[axis_at] // parts).reshape((-1,) + (1,) * (len(shape) - axis_at - 1))

    level = one(*split[0])
    for cut in split[1:]:
        level = level * one(*cut)
    return level


def normal_values(stream_key, shape, scale, most, cuts=(), dtype=jnp.bfloat16):
    loudness = level_of(stream_key, shape, cuts, -0.22, 0.18) if cuts else 1.0
    result = jax.random.normal(stream_key, shape, jnp.float32) * scale * loudness
    return jnp.minimum(jnp.maximum(result, -most), most).astype(dtype)


def setup_inputs(seed: int = 0) -> dict:
    key_of = jax.random.split(jax.random.key(seed), 13)
    return {
        "stream": normal_values(key_of[0], (FRAMES, ROWS, COLS, D), 1.0, 6.0, ((0, 16), (1, 2))),
        "queries": normal_values(key_of[1], (FRAMES, ROWS, COLS, D), 1.0, 6.0, ((0, 16), (1, 2))),
        "keys": normal_values(key_of[2], (FRAMES, ROWS, COLS, D), 1.0, 6.0, ((0, 16), (1, 2))),
        "values": normal_values(key_of[3], (FRAMES, ROWS, COLS, D), 1.0, 6.0, ((0, 16), (1, 2))),
        "state_in": normal_values(key_of[4], (HEADS, HEAD_DIM, HEAD_DIM), 20.0, 120.0, (), jnp.float32),
        "keysum_in": jnp.clip(jnp.exp(jax.random.uniform(key_of[5], (HEADS, HEAD_DIM), jnp.float32, math.log(100.0), math.log(1000.0))), 100.0, 1000.0),
        "attn_gate": jnp.clip(jnp.exp(jax.random.uniform(key_of[6], (D,), jnp.float32, math.log(2.0), math.log(20.0))), 2.0, 20.0),
        "ffn_shift": normal_values(key_of[7], (D,), 0.5, 3.0, (), jnp.float32),
        "ffn_scale": normal_values(key_of[8], (D,), 0.5, 3.0, (), jnp.float32),
        "w_up": normal_values(key_of[9], (D, 2 * FW), D ** -0.5, 0.125, ((0, 16),)),
        "conv_weight": normal_values(key_of[10], (3, 3, 2 * FW), 9 ** -0.5, 2.0, (), jnp.float32),
        "conv_bias": normal_values(key_of[11], (2 * FW,), 0.5, 3.0, (), jnp.float32),
    }


EPS = 1e-06

def depthwise(up, conv_weight, conv_bias):
    padded = jnp.pad(up.astype(jnp.float32), ((1, 1), (1, 1), (0, 0)))
    total = jnp.zeros(up.shape, jnp.float32) + conv_bias
    for above in range(3):
        for across in range(3):
            total = total + conv_weight[above, across] * padded[above:above + ROWS, across:across + COLS]
    return total

def reference(stream, queries, keys, values, state_in, keysum_in, attn_gate, ffn_shift, ffn_scale, w_up, conv_weight, conv_bias):
    heads = state_in.shape[0]
    head_size = state_in.shape[1]
    count = ROWS * COLS
    weight_full = w_up.astype(jnp.float32)
    high = lax.Precision.HIGHEST

    def frame_step(carry, frame):
        state, keysum = carry
        frame_stream, frame_query, frame_keys_in, frame_values = frame
        key_feat = jnp.maximum(frame_keys_in.astype(jnp.float32), 0.0).reshape(count, heads, head_size)
        value_rows = frame_values.astype(jnp.float32).reshape(count, heads, head_size)
        query_feat = jnp.maximum(frame_query.astype(jnp.float32), 0.0).reshape(count, heads, head_size)
        state = state + jnp.einsum('tha,thb->hab', key_feat, value_rows, precision=high)
        keysum = keysum + lax.optimization_barrier(jnp.sum(key_feat, axis=0))
        numerator = jnp.einsum('the,hed->thd', query_feat, state, precision=high)
        denominator = jnp.einsum('the,he->th', query_feat, keysum, precision=high) + 1.0
        attn = (numerator / denominator[..., None]).reshape(ROWS, COLS, heads * head_size)
        mixed = (frame_stream.astype(jnp.float32) + attn_gate * attn).astype(jnp.bfloat16)
        mixed_f = lax.optimization_barrier(mixed).astype(jnp.float32)
        mean = lax.optimization_barrier(jnp.mean(mixed_f, axis=-1, keepdims=True))
        centered = mixed_f - mean
        variance = lax.optimization_barrier(jnp.mean(centered * centered, axis=-1, keepdims=True))
        normed = centered * lax.rsqrt(variance + EPS)
        modulated = (normed * (1.0 + ffn_scale) + ffn_shift).astype(jnp.bfloat16)
        modulated = lax.optimization_barrier(modulated).astype(jnp.float32)
        up = jnp.dot(modulated.reshape(count, -1), weight_full, precision=high).astype(jnp.bfloat16)
        up = lax.optimization_barrier(up).reshape(ROWS, COLS, 2 * FW)
        conv = depthwise(up, conv_weight, conv_bias)
        hidden = (conv[..., :FW] * jax.nn.silu(conv[..., FW:])).astype(jnp.bfloat16)
        return ((state, keysum), (mixed, hidden))
    carry = (state_in.astype(jnp.float32), keysum_in.astype(jnp.float32))
    _, (mixed, hidden) = lax.scan(frame_step, carry, (stream, queries, keys, values))
    return (mixed, hidden)
```

```python
import functools

import jax
import jax.numpy as jnp
from jax import lax
from jax.experimental import pallas as pl
from jax.experimental.pallas import tpu as pltpu
from jax.sharding import PartitionSpec as P

EPS = 1e-06
LANES = 128
BF16 = jnp.bfloat16
F32 = jnp.float32
PARAMS = pltpu.CompilerParams(
    dimension_semantics=("arbitrary",), vmem_limit_bytes=56 * 1024 * 1024
)


def up_to(size, step):
    return -(-size // step) * step


def kv_kernel(heads, head_size, parts, place, k_ref, v_ref, *refs):
    outs, held = refs[:parts], refs[parts]
    tokens = k_ref.shape[1]
    each = heads // parts
    feats = jnp.maximum(k_ref[0], 0)
    vals = v_ref[0]
    ones = jnp.ones((tokens, LANES - head_size), BF16)
    for h in range(heads):
        lanes = slice(h * head_size, (h + 1) * head_size)
        right = jnp.concatenate([vals[:, lanes], ones], axis=1)
        held[h] = lax.dot_general(
            feats[:, lanes],
            right,
            (((0,), (0,)), ((), ())),
            preferred_element_type=F32,
        ).astype(BF16)
    for part in range(parts):
        slot = lax.rem(part - place[0] + parts, parts)
        for k in range(parts):

            @pl.when(slot == k)
            def _():
                outs[k][0] = held[part * each : (part + 1) * each]


def attn_kernel(
    heads, head_size, parts, deep, deep_pad, cols, place, q_ref, s_ref, in_ref, gate, shift, scale, *refs
):
    gathered = refs[:parts]
    mixed_ref, x_ref = refs[parts], refs[parts + 1]
    edges = refs[parts + 2 : -1]
    attn = refs[-1]
    tokens, width = q_ref.shape[1:]
    each = heads // parts
    feats = jnp.maximum(q_ref[0], 0)
    for h in range(heads):
        part, i = divmod(h, each)
        slot = lax.rem(place[0] - part + parts, parts)
        state = gathered[0][0, i].astype(F32)
        for k in range(1, parts):
            state = jnp.where(slot == k, gathered[k][0, i].astype(F32), state)
        state = state + in_ref[h]
        high = state.astype(BF16)
        low = (state - high.astype(F32)).astype(BF16)
        lanes = slice(h * head_size, (h + 1) * head_size)
        both = jnp.dot(
            feats[:, lanes], jnp.concatenate([high, low], axis=1), preferred_element_type=F32
        )
        sums = both[:, :LANES] + both[:, LANES:]
        below = sums[:, head_size : head_size + 1] + 1.0
        attn[:, lanes] = sums[:, :head_size] * (1.0 / below)
    mixed = (s_ref[0].astype(F32) + gate[...] * attn[...]).astype(BF16)
    mixed_ref[0] = mixed
    wide = mixed.astype(F32)
    mean = jnp.sum(wide, axis=1, keepdims=True) * (1.0 / width)
    centered = wide - mean
    variance = jnp.sum(centered * centered, axis=1, keepdims=True) * (1.0 / width)
    normed = centered * lax.rsqrt(variance + EPS)
    modulated = (normed * (1.0 + scale[...]) + shift[...]).astype(BF16)
    blank = jnp.zeros((tokens, deep_pad - deep), BF16)
    pieces = []
    for t in range(width // deep):
        pieces += [modulated[:, t * deep : (t + 1) * deep], blank]
    rows = jnp.concatenate(pieces, axis=1)
    x_ref[0] = rows
    if len(edges) == 1:
        edges[0][0] = jnp.where(place[0] == 0, rows[tokens - cols :], rows[:cols])
    else:
        edges[0][0] = rows[:cols]
        edges[1][0] = rows[tokens - cols :]


def ffn_kernel(frames, rows, cols, halos, place, x_ref, *refs):
    halo = refs[:halos]
    wv, wg, cv, cg, bv, bg, out, xs, left, mid, right = refs[halos:]
    own = frames * rows * cols
    edge = frames * cols

    @pl.when(pl.program_id(0) == 0)
    def _():
        xs[:own] = x_ref[...]
        for k in range(halos):
            xs[own + k * edge : own + (k + 1) * edge] = halo[k][...]

    total = own + halos * edge
    at = lax.rem(lax.broadcasted_iota(jnp.int32, (total, 1), 0), cols)
    first, last = at == 0, at == cols - 1
    above_ok = place[0] > 0
    for side, (w, c, b) in enumerate(((wv, cv, bv), (wg, cg, bg))):
        up = jnp.dot(xs[...], w[...], preferred_element_type=F32).astype(BF16).astype(F32)
        mid[side] = up
        left[side] = jnp.where(first, 0.0, pltpu.roll(up, 1, 0))
        right[side] = jnp.where(last, 0.0, pltpu.roll(up, total - 1, 0))

    def row_of(side, f, r):
        if 0 <= r < rows:
            at = slice((f * rows + r) * cols, (f * rows + r + 1) * cols)
            return [ref[side, at] for ref in (left, mid, right)]
        if halos == 1:
            at = slice(own + f * cols, own + (f + 1) * cols)
            used = above_ok if r < 0 else jnp.logical_not(above_ok)
            return [jnp.where(used, ref[side, at], 0.0) for ref in (left, mid, right)]
        start = own + (0 if r < 0 else edge) + f * cols
        at = slice(start, start + cols)
        return [ref[side, at] for ref in (left, mid, right)]

    for f in range(frames):
        for r in range(rows):
            convs = []
            for side, (c, b) in enumerate(((cv, bv), (cg, bg))):
                total_row = jnp.broadcast_to(b[...], (cols, b.shape[1]))
                for above in range(3):
                    three = row_of(side, f, r + above - 1)
                    for across in range(3):
                        k = above * 3 + across
                        total_row = total_row + c[k : k + 1] * three[across]
                convs.append(total_row)
            value, gate = convs
            at = slice((f * rows + r) * cols, (f * rows + r + 1) * cols)
            out[at] = (value * (gate * (1.0 / (1.0 + jnp.exp(-gate))))).astype(BF16)


def local(
    stream,
    queries,
    keys,
    values,
    state_in,
    keysum_in,
    attn_gate,
    ffn_shift,
    ffn_scale,
    w_up,
    conv_weight,
    conv_bias,
):
    frames, rows, cols, width = stream.shape
    heads, head_size = keysum_in.shape
    tokens = rows * cols
    parts = lax.axis_size("space")
    peers = lax.axis_size("tm")
    each = heads // parts
    half = w_up.shape[1] // 2
    block = 2 * LANES
    half_pad = up_to(half, block)
    deep = w_up.shape[0]
    deep_pad = up_to(deep, 8)
    depth = peers * deep_pad
    place = lax.axis_index("space").astype(jnp.int32).reshape(1)

    def round_space(array, k):
        return lax.ppermute(array, "space", [(i, (i + k) % parts) for i in range(parts)])

    def filled(array):
        side = jnp.zeros(array.shape[:-1] + (half_pad - half,), array.dtype)
        return jnp.concatenate([array[..., :half], side, array[..., half:], side], axis=-1)

    weights = jnp.pad(filled(w_up), ((0, deep_pad - deep), (0, 0)))
    weights = lax.all_gather(weights, "tm", axis=0).reshape(depth, 2 * half_pad)
    taps = filled(conv_weight.reshape(9, 2 * half))
    bias = filled(conv_bias.reshape(1, 2 * half))

    def frame_block(*shape):
        return pl.BlockSpec((1,) + shape, lambda f, _: (f,) + (0,) * len(shape))

    def whole(*shape):
        return pl.BlockSpec(shape, lambda f, _: (0,) * len(shape))

    flat = (frames, tokens, width)
    part_shape = (each, head_size, LANES)
    sums = pl.pallas_call(
        functools.partial(kv_kernel, heads, head_size, parts),
        grid_spec=pltpu.PrefetchScalarGridSpec(
            num_scalar_prefetch=1,
            grid=(frames,),
            in_specs=[frame_block(tokens, width)] * 2,
            out_specs=[frame_block(*part_shape)] * parts,
            scratch_shapes=[pltpu.VMEM((heads, head_size, LANES), BF16)],
        ),
        out_shape=[jax.ShapeDtypeStruct((frames,) + part_shape, BF16)] * parts,
        compiler_params=PARAMS,
        name="frame_sums",
    )(place, keys.reshape(flat), values.reshape(flat))
    mine = sums[0].astype(F32)
    for k in range(1, parts):
        mine = mine + round_space(sums[k], k).astype(F32)
    running = jnp.sum(mine, axis=0)
    prior = jnp.zeros_like(running)
    step = 1
    while step < peers:
        got = lax.ppermute(
            running.astype(BF16), "tm", [(i, i + step) for i in range(peers - step)]
        ).astype(F32)
        prior = prior + got
        running = running + got
        step *= 2
    states = (prior + jnp.cumsum(mine, axis=0)).astype(BF16)
    gathered = [states] + [round_space(states, k) for k in range(1, parts)]
    start = jnp.concatenate(
        [state_in, jnp.broadcast_to(keysum_in[..., None], (heads, head_size, LANES - head_size))],
        axis=-1,
    )
    halos = 1 if parts == 2 else 2
    mixed, x, *edges = pl.pallas_call(
        functools.partial(attn_kernel, heads, head_size, parts, deep, deep_pad, cols),
        grid_spec=pltpu.PrefetchScalarGridSpec(
            num_scalar_prefetch=1,
            grid=(frames,),
            in_specs=[frame_block(tokens, width)] * 2
            + [whole(heads, head_size, LANES)]
            + [whole(1, width)] * 3
            + [frame_block(*part_shape)] * parts,
            out_specs=[frame_block(tokens, width), frame_block(tokens, depth)]
            + [frame_block(cols, depth)] * halos,
            scratch_shapes=[pltpu.VMEM((tokens, width), F32)],
        ),
        out_shape=[
            jax.ShapeDtypeStruct(flat, BF16),
            jax.ShapeDtypeStruct((frames, tokens, depth), BF16),
        ]
        + [jax.ShapeDtypeStruct((frames, cols, depth), BF16)] * halos,
        compiler_params=PARAMS,
        name="attention",
    )(
        place,
        queries.reshape(flat),
        stream.reshape(flat),
        start,
        attn_gate.reshape(1, width),
        ffn_shift.reshape(1, width),
        ffn_scale.reshape(1, width),
        *gathered,
    )
    if halos == 1:
        around = [round_space(edges[0], 1)]
    else:
        around = [
            lax.ppermute(edges[1], "space", [(i, i + 1) for i in range(parts - 1)]),
            lax.ppermute(edges[0], "space", [(i + 1, i) for i in range(parts - 1)]),
        ]
    blocks = half_pad // block
    own = frames * tokens
    total = own + halos * frames * cols

    def column(height, shift):
        return pl.BlockSpec((height, block), lambda j, _: (0, j + shift))

    hidden = pl.pallas_call(
        functools.partial(ffn_kernel, frames, rows, cols, halos),
        grid_spec=pltpu.PrefetchScalarGridSpec(
            num_scalar_prefetch=1,
            grid=(blocks,),
            in_specs=[whole(own, depth)]
            + [whole(frames * cols, depth)] * halos
            + [column(depth, 0), column(depth, blocks)]
            + [column(9, 0), column(9, blocks), column(1, 0), column(1, blocks)],
            out_specs=column(own, 0),
            scratch_shapes=[pltpu.VMEM((total, depth), BF16)]
            + [pltpu.VMEM((2, total, block), F32)] * 3,
        ),
        out_shape=jax.ShapeDtypeStruct((own, half), BF16),
        compiler_params=PARAMS,
        name="mix_ffn",
    )(
        place,
        x.reshape(own, depth),
        *[a.reshape(frames * cols, depth) for a in around],
        weights,
        weights,
        taps,
        taps,
        bias,
        bias,
    )
    return mixed.reshape(stream.shape), hidden.reshape(frames, rows, cols, half)


def solution(mesh):
    placed = (
        P("tm", "space", None, None),
        P("tm", "space", None, None),
        P("tm", "space", None, None),
        P("tm", "space", None, None),
        P(),
        P(),
        P(),
        P(),
        P(),
        P("tm", None),
        P(),
        P(),
    )
    return jax.shard_map(
        local,
        mesh=mesh,
        in_specs=placed,
        out_specs=(P("tm", "space", None, None), P("tm", "space", None, None)),
        check_vma=False,
    )
```

```python
import functools

import jax
import jax.numpy as jnp
from jax import lax
from jax.experimental import pallas as pl
from jax.experimental.pallas import tpu as pltpu
from jax.sharding import PartitionSpec as P

EPS = 1e-06
LANES = 128
SUBLANES = 8
BF16 = jnp.bfloat16
F32 = jnp.float32
PARAMS = pltpu.CompilerParams(
    dimension_semantics=("arbitrary",), vmem_limit_bytes=56 * 1024 * 1024
)


def up_to(size, step):
    return -(-size // step) * step


def kv_kernel(heads, head_size, parts, place, k_ref, v_ref, *refs):
    outs, held = refs[:parts], refs[parts]
    tokens = k_ref.shape[1]
    each = heads // parts
    feats = jnp.maximum(k_ref[0], 0)
    vals = v_ref[0]
    ones = jnp.ones((tokens, LANES - head_size), BF16)
    for h in range(heads):
        lanes = slice(h * head_size, (h + 1) * head_size)
        right = jnp.concatenate([vals[:, lanes], ones], axis=1)
        held[h] = lax.dot_general(
            feats[:, lanes],
            right,
            (((0,), (0,)), ((), ())),
            preferred_element_type=F32,
        ).astype(BF16)
    for part in range(parts):
        slot = lax.rem(part - place[0] + parts, parts)
        for k in range(parts):

            @pl.when(slot == k)
            def _():
                outs[k][0] = held[part * each : (part + 1) * each]


def attn_kernel(
    heads, head_size, parts, deep, deep_pad, cols, place, q_ref, s_ref, in_ref, gate, shift, scale, *refs
):
    gathered = refs[:parts]
    mixed_ref, x_ref = refs[parts], refs[parts + 1]
    edges = refs[parts + 2 : -1]
    attn = refs[-1]
    tokens, width = q_ref.shape[1:]
    each = heads // parts
    feats = jnp.maximum(q_ref[0], 0)
    for h in range(heads):
        part, i = divmod(h, each)
        slot = lax.rem(place[0] - part + parts, parts)
        state = gathered[0][0, i].astype(F32)
        for k in range(1, parts):
            state = jnp.where(slot == k, gathered[k][0, i].astype(F32), state)
        state = state + in_ref[h]
        high = state.astype(BF16)
        low = (state - high.astype(F32)).astype(BF16)
        lanes = slice(h * head_size, (h + 1) * head_size)
        both = jnp.dot(
            feats[:, lanes], jnp.concatenate([high, low], axis=1), preferred_element_type=F32
        )
        sums = both[:, :LANES] + both[:, LANES:]
        below = sums[:, head_size : head_size + 1] + 1.0
        attn[:, lanes] = sums[:, :head_size] * (1.0 / below)
    mixed = (s_ref[0].astype(F32) + gate[...] * attn[...]).astype(BF16)
    mixed_ref[0] = mixed
    wide = mixed.astype(F32)
    mean = jnp.sum(wide, axis=1, keepdims=True) * (1.0 / width)
    centered = wide - mean
    variance = jnp.sum(centered * centered, axis=1, keepdims=True) * (1.0 / width)
    normed = centered * lax.rsqrt(variance + EPS)
    modulated = (normed * (1.0 + scale[...]) + shift[...]).astype(BF16)
    blank = jnp.zeros((tokens, deep_pad - deep), BF16)
    pieces = []
    for t in range(width // deep):
        pieces += [modulated[:, t * deep : (t + 1) * deep], blank]
    rows = jnp.concatenate(pieces, axis=1)
    x_ref[0] = rows
    if len(edges) == 1:
        edges[0][0] = jnp.where(place[0] == 0, rows[tokens - cols :], rows[:cols])
    else:
        edges[0][0] = rows[:cols]
        edges[1][0] = rows[tokens - cols :]


def pack_kernel(half, deep, w_ref, out_ref):
    height, width = out_ref.shape
    at = lax.broadcasted_iota(jnp.int32, (height, 1), 0) + pl.program_id(0) * height
    rows = jnp.where(at < deep, w_ref[...], jnp.zeros((), BF16))
    for k in range(width // (2 * LANES)):
        for side in range(2):
            first, end = k * LANES, min((k + 1) * LANES, half)
            piece = rows[:, side * half + first : side * half + end]
            if end - first < LANES:
                blank = jnp.zeros((height, LANES - (end - first)), BF16)
                piece = jnp.concatenate([piece, blank], axis=1)
            out_ref[:, (2 * k + side) * LANES : (2 * k + side + 1) * LANES] = piece


def ffn_kernel(frames, rows, cols, halos, place, x_ref, *refs):
    halo = refs[:halos]
    w_ref, taps, bias, out, xs, upa, upb, laid = refs[halos:]
    own = frames * rows * cols
    edge = frames * cols
    per = cols // SUBLANES

    @pl.when(pl.program_id(0) == 0)
    def _():
        xs[:own] = x_ref[...]
        for k in range(halos):
            xs[own + k * edge : own + (k + 1) * edge] = halo[k][...]

    has_above = place[0] > 0
    spot = lax.broadcasted_iota(jnp.int32, (SUBLANES, LANES), 0)

    def product(k, up):
        both = jnp.dot(
            xs[...], w_ref[:, 2 * k * LANES : 2 * (k + 1) * LANES], preferred_element_type=F32
        )
        up[0] = both[:, :LANES]
        up[1] = both[:, LANES:]

    def row_of(up, side, f, r):
        if 0 <= r < rows:
            first, used = (f * rows + r) * cols, None
        elif halos == 1:
            first = own + f * cols
            used = has_above if r < 0 else jnp.logical_not(has_above)
        else:
            first, used = own + (0 if r < 0 else edge) + f * cols, None
        row = [up[side, pl.ds(first + i, SUBLANES, stride=per), :] for i in range(per)]
        return row if used is None else [jnp.where(used, part, 0.0) for part in row]

    def conv(k, up):
        for f in range(frames):
            for r in range(rows):
                pair = []
                for side in range(2):
                    lanes = slice((2 * k + side) * LANES, (2 * k + side + 1) * LANES)
                    three = [row_of(up, side, f, r + a) for a in (-1, 0, 1)]
                    left, mid, right = (
                        [
                            sum(
                                taps[3 * a + b : 3 * a + b + 1, lanes] * three[a][i]
                                for a in range(3)
                            )
                            for i in range(per)
                        ]
                        for b in range(3)
                    )
                    before = jnp.where(spot == 0, 0.0, pltpu.roll(left[per - 1], 1, 0))
                    after = jnp.where(
                        spot == SUBLANES - 1, 0.0, pltpu.roll(right[0], SUBLANES - 1, 0)
                    )
                    left = [before] + left[: per - 1]
                    right = right[1:] + [after]
                    pair.append(
                        [bias[:, lanes] + mid[i] + left[i] + right[i] for i in range(per)]
                    )
                first = (f * rows + r) * cols
                for i in range(per):
                    half = 0.5 * pair[1][i]
                    laid[k, pl.ds(first + i, SUBLANES, stride=per), :] = pair[0][i] * (
                        half + half * jnp.tanh(half)
                    )
                out[first : first + cols, k * LANES : (k + 1) * LANES] = laid[
                    k, first : first + cols
                ].astype(BF16)

    product(0, upa)
    product(1, upb)
    conv(0, upa)
    conv(1, upb)


def earlier(totals, peers):
    me = lax.axis_index("tm")
    rows = totals.shape[0]

    def swap(array, bit):
        pairs = [(i, i ^ bit) for i in range(peers)]
        return lax.ppermute(array.astype(BF16), "tm", pairs).astype(F32)

    def joined(mine, other, upper):
        both = jnp.stack([jnp.where(upper, other, mine), jnp.where(upper, mine, other)])
        return both.reshape((-1,) + mine.shape[1:])

    odd, second = lax.rem(me, 2) == 1, lax.rem(me // 2, 2) == 1
    near = swap(totals, 1)
    pair = (totals + near).reshape(2, rows // 2, -1)
    pair = jnp.where(odd, pair[1], pair[0])
    next_pair = swap(pair, 2)
    four = (pair + next_pair).reshape(2, rows // 4, -1)
    running = jnp.where(second, four[1], four[0])
    prior = jnp.zeros_like(running)
    step = 4
    while step < peers:
        got = lax.ppermute(
            running.astype(BF16), "tm", [(i, i + step) for i in range(peers - step)]
        ).astype(F32)
        prior, running = prior + got, running + got
        step *= 2
    prior = joined(prior, swap(prior, 2), second)
    prior = prior + jnp.where(second, next_pair, 0.0)
    prior = joined(prior, swap(prior, 1), odd)
    return prior + jnp.where(odd, near, 0.0)


def local(
    stream,
    queries,
    keys,
    values,
    state_in,
    keysum_in,
    attn_gate,
    ffn_shift,
    ffn_scale,
    w_up,
    conv_weight,
    conv_bias,
):
    frames, rows, cols, width = stream.shape
    heads, head_size = keysum_in.shape
    tokens = rows * cols
    parts = lax.axis_size("space")
    peers = lax.axis_size("tm")
    each = heads // parts
    half = w_up.shape[1] // 2
    half_pad = up_to(half, 2 * LANES)
    deep = w_up.shape[0]
    deep_pad = up_to(deep, 8)
    depth = peers * deep_pad
    place = lax.axis_index("space").astype(jnp.int32).reshape(1)

    def round_space(array, k):
        return lax.ppermute(array, "space", [(i, (i + k) % parts) for i in range(parts)])

    def interleaved(array):
        both = array.reshape(array.shape[0], 2, half)
        both = jnp.pad(both, ((0, 0), (0, 0), (0, half_pad - half)))
        both = both.reshape(array.shape[0], 2, half_pad // LANES, LANES)
        return both.transpose(0, 2, 1, 3).reshape(array.shape[0], 2 * half_pad)

    height = 48 if deep_pad % 48 == 0 else deep_pad
    weights = pl.pallas_call(
        functools.partial(pack_kernel, half, deep),
        grid=(deep_pad // height,),
        in_specs=[pl.BlockSpec((height, 2 * half), lambda i: (i, 0))],
        out_specs=pl.BlockSpec((height, 2 * half_pad), lambda i: (i, 0)),
        out_shape=jax.ShapeDtypeStruct((deep_pad, 2 * half_pad), BF16),
        compiler_params=PARAMS,
        name="pack",
    )(w_up)
    weights = lax.all_gather(weights, "tm", axis=0).reshape(depth, 2 * half_pad)
    taps = interleaved(conv_weight.reshape(9, 2 * half))
    bias = interleaved(conv_bias.reshape(1, 2 * half))

    def frame_block(*shape):
        return pl.BlockSpec((1,) + shape, lambda f, _: (f,) + (0,) * len(shape))

    def whole(*shape):
        return pl.BlockSpec(shape, lambda f, _: (0,) * len(shape))

    flat = (frames, tokens, width)
    part_shape = (each, head_size, LANES)
    sums = pl.pallas_call(
        functools.partial(kv_kernel, heads, head_size, parts),
        grid_spec=pltpu.PrefetchScalarGridSpec(
            num_scalar_prefetch=1,
            grid=(frames,),
            in_specs=[frame_block(tokens, width)] * 2,
            out_specs=[frame_block(*part_shape)] * parts,
            scratch_shapes=[pltpu.VMEM((heads, head_size, LANES), BF16)],
        ),
        out_shape=[jax.ShapeDtypeStruct((frames,) + part_shape, BF16)] * parts,
        compiler_params=PARAMS,
        name="frame_sums",
    )(place, keys.reshape(flat), values.reshape(flat))
    mine = sums[0].astype(F32)
    for k in range(1, parts):
        mine = mine + round_space(sums[k], k).astype(F32)
    prior = earlier(jnp.sum(mine, axis=0).reshape(each * head_size, LANES), peers)
    prior = prior.reshape(part_shape)
    states = (prior + jnp.cumsum(mine, axis=0)).astype(BF16)
    gathered = [states] + [round_space(states, k) for k in range(1, parts)]
    start = jnp.concatenate(
        [state_in, jnp.broadcast_to(keysum_in[..., None], (heads, head_size, LANES - head_size))],
        axis=-1,
    )
    halos = 1 if parts == 2 else 2
    mixed, x, *edges = pl.pallas_call(
        functools.partial(attn_kernel, heads, head_size, parts, deep, deep_pad, cols),
        grid_spec=pltpu.PrefetchScalarGridSpec(
            num_scalar_prefetch=1,
            grid=(frames,),
            in_specs=[frame_block(tokens, width)] * 2
            + [whole(heads, head_size, LANES)]
            + [whole(1, width)] * 3
            + [frame_block(*part_shape)] * parts,
            out_specs=[frame_block(tokens, width), frame_block(tokens, depth)]
            + [frame_block(cols, depth)] * halos,
            scratch_shapes=[pltpu.VMEM((tokens, width), F32)],
        ),
        out_shape=[
            jax.ShapeDtypeStruct(flat, BF16),
            jax.ShapeDtypeStruct((frames, tokens, depth), BF16),
        ]
        + [jax.ShapeDtypeStruct((frames, cols, depth), BF16)] * halos,
        compiler_params=PARAMS,
        name="attention",
    )(
        place,
        queries.reshape(flat),
        stream.reshape(flat),
        start,
        attn_gate.reshape(1, width),
        ffn_shift.reshape(1, width),
        ffn_scale.reshape(1, width),
        *gathered,
    )
    if halos == 1:
        around = [round_space(edges[0], 1)]
    else:
        around = [
            lax.ppermute(edges[1], "space", [(i, i + 1) for i in range(parts - 1)]),
            lax.ppermute(edges[0], "space", [(i + 1, i) for i in range(parts - 1)]),
        ]
    own = frames * tokens
    total = own + halos * frames * cols

    def column(rows_in, wide):
        return pl.BlockSpec((rows_in, wide), lambda j, _: (0, j))

    hidden = pl.pallas_call(
        functools.partial(ffn_kernel, frames, rows, cols, halos),
        grid_spec=pltpu.PrefetchScalarGridSpec(
            num_scalar_prefetch=1,
            grid=(half_pad // (2 * LANES),),
            in_specs=[whole(own, depth)]
            + [whole(frames * cols, depth)] * halos
            + [column(depth, 4 * LANES), column(9, 4 * LANES), column(1, 4 * LANES)],
            out_specs=column(own, 2 * LANES),
            scratch_shapes=[pltpu.VMEM((total, depth), BF16)]
            + [pltpu.VMEM((2, total, LANES), F32)] * 2
            + [pltpu.VMEM((2, own, LANES), F32)],
        ),
        out_shape=jax.ShapeDtypeStruct((own, half), BF16),
        compiler_params=PARAMS,
        name="mix_ffn",
    )(
        place,
        x.reshape(own, depth),
        *[a.reshape(frames * cols, depth) for a in around],
        weights,
        taps,
        bias,
    )
    return mixed.reshape(stream.shape), hidden.reshape(frames, rows, cols, half)


def solution(mesh):
    placed = (
        P("tm", "space", None, None),
        P("tm", "space", None, None),
        P("tm", "space", None, None),
        P("tm", "space", None, None),
        P(),
        P(),
        P(),
        P(),
        P(),
        P("tm", None),
        P(),
        P(),
    )
    return jax.shard_map(
        local,
        mesh=mesh,
        in_specs=placed,
        out_specs=(P("tm", "space", None, None), P("tm", "space", None, None)),
        check_vma=False,
    )
```

```python
import functools

import jax
import jax.numpy as jnp
from jax import lax
from jax.experimental import pallas as pl
from jax.experimental.pallas import tpu as pltpu
from jax.sharding import PartitionSpec as P

EPS = 1e-06
LANES = 128
SUBLANES = 8
BF16 = jnp.bfloat16
F32 = jnp.float32
PARAMS = pltpu.CompilerParams(
    dimension_semantics=("arbitrary",), vmem_limit_bytes=56 * 1024 * 1024
)


def up_to(size, step):
    return -(-size // step) * step


def kv_kernel(heads, head_size, parts, place, k_ref, v_ref, *refs):
    outs, held = refs[:parts], refs[parts]
    tokens = k_ref.shape[1]
    each = heads // parts
    feats = jnp.maximum(k_ref[0], 0)
    vals = v_ref[0]
    ones = jnp.ones((tokens, LANES - head_size), BF16)
    for h in range(heads):
        lanes = slice(h * head_size, (h + 1) * head_size)
        right = jnp.concatenate([vals[:, lanes], ones], axis=1)
        held[h] = lax.dot_general(
            feats[:, lanes],
            right,
            (((0,), (0,)), ((), ())),
            preferred_element_type=F32,
        ).astype(BF16)
    for part in range(parts):
        slot = lax.rem(part - place[0] + parts, parts)
        for k in range(parts):

            @pl.when(slot == k)
            def _():
                outs[k][0] = held[part * each : (part + 1) * each]


def attn_kernel(
    heads, head_size, parts, deep, deep_pad, cols, place, q_ref, s_ref, in_ref, gate, shift, scale, *refs
):
    gathered = refs[:parts]
    mixed_ref, x_ref = refs[parts], refs[parts + 1]
    edges = refs[parts + 2 : -1]
    attn = refs[-1]
    tokens, width = q_ref.shape[1:]
    each = heads // parts
    feats = jnp.maximum(q_ref[0], 0)
    for h in range(heads):
        part, i = divmod(h, each)
        slot = lax.rem(place[0] - part + parts, parts)
        state = gathered[0][0, i].astype(F32)
        for k in range(1, parts):
            state = jnp.where(slot == k, gathered[k][0, i].astype(F32), state)
        state = state + in_ref[h]
        high = state.astype(BF16)
        low = (state - high.astype(F32)).astype(BF16)
        lanes = slice(h * head_size, (h + 1) * head_size)
        both = jnp.dot(
            feats[:, lanes], jnp.concatenate([high, low], axis=1), preferred_element_type=F32
        )
        sums = both[:, :LANES] + both[:, LANES:]
        below = sums[:, head_size : head_size + 1] + 1.0
        attn[:, lanes] = sums[:, :head_size] * (1.0 / below)
    mixed = (s_ref[0].astype(F32) + gate[...] * attn[...]).astype(BF16)
    mixed_ref[0] = mixed
    wide = mixed.astype(F32)
    mean = jnp.sum(wide, axis=1, keepdims=True) * (1.0 / width)
    centered = wide - mean
    variance = jnp.sum(centered * centered, axis=1, keepdims=True) * (1.0 / width)
    normed = centered * lax.rsqrt(variance + EPS)
    modulated = (normed * (1.0 + scale[...]) + shift[...]).astype(BF16)
    blank = jnp.zeros((tokens, deep_pad - deep), BF16)
    pieces = []
    for t in range(width // deep):
        pieces += [modulated[:, t * deep : (t + 1) * deep], blank]
    rows = jnp.concatenate(pieces, axis=1)
    x_ref[0] = rows
    if len(edges) == 1:
        edges[0][0] = jnp.where(place[0] == 0, rows[tokens - cols :], rows[:cols])
    else:
        edges[0][0] = rows[:cols]
        edges[1][0] = rows[tokens - cols :]


def pack_kernel(half, deep, w_ref, out_ref):
    height, width = out_ref.shape
    at = lax.broadcasted_iota(jnp.int32, (height, 1), 0) + pl.program_id(0) * height
    rows = jnp.where(at < deep, w_ref[...], jnp.zeros((), BF16))
    for k in range(width // (2 * LANES)):
        for side in range(2):
            first, end = k * LANES, min((k + 1) * LANES, half)
            piece = rows[:, side * half + first : side * half + end]
            if end - first < LANES:
                blank = jnp.zeros((height, LANES - (end - first)), BF16)
                piece = jnp.concatenate([piece, blank], axis=1)
            out_ref[:, (2 * k + side) * LANES : (2 * k + side + 1) * LANES] = piece


def ffn_kernel(frames, rows, cols, halos, place, x_ref, *refs):
    w_ref, taps, bias, out, upa, upb, rawa, rawb, laid = refs
    own = frames * rows * cols
    edge = frames * cols
    per = cols // SUBLANES

    has_above = place[0] > 0
    spot = lax.broadcasted_iota(jnp.int32, (SUBLANES, LANES), 0)

    def product(k, up, raw):
        both = jnp.dot(
            x_ref[...], w_ref[:, 2 * k * LANES : 2 * (k + 1) * LANES], preferred_element_type=F32
        )
        raw[0] = both[:, :LANES]
        raw[1] = both[:, LANES:]
        for side in range(2):
            for first in range(0, both.shape[0], cols):
                for i in range(per):
                    at = slice(first + i * SUBLANES, first + (i + 1) * SUBLANES)
                    up[side, at] = raw[side, pl.ds(first + i, SUBLANES, stride=per), :]

    def row_of(up, side, f, r):
        if 0 <= r < rows:
            first, used = (f * rows + r) * cols, None
        elif halos == 1:
            first = own + f * cols
            used = has_above if r < 0 else jnp.logical_not(has_above)
        else:
            first, used = own + (0 if r < 0 else edge) + f * cols, None
        row = [
            up[side, first + i * SUBLANES : first + (i + 1) * SUBLANES] for i in range(per)
        ]
        return row if used is None else [jnp.where(used, part, 0.0) for part in row]

    def conv(k, up):
        for f in range(frames):
            for r in range(rows):
                pair = []
                for side in range(2):
                    lanes = slice((2 * k + side) * LANES, (2 * k + side + 1) * LANES)
                    three = [row_of(up, side, f, r + a) for a in (-1, 0, 1)]
                    left, mid, right = (
                        [
                            sum(
                                taps[3 * a + b : 3 * a + b + 1, lanes] * three[a][i]
                                for a in range(3)
                            )
                            for i in range(per)
                        ]
                        for b in range(3)
                    )
                    before = jnp.where(spot == 0, 0.0, pltpu.roll(left[per - 1], 1, 0))
                    after = jnp.where(
                        spot == SUBLANES - 1, 0.0, pltpu.roll(right[0], SUBLANES - 1, 0)
                    )
                    left = [before] + left[: per - 1]
                    right = right[1:] + [after]
                    pair.append(
                        [bias[:, lanes] + mid[i] + left[i] + right[i] for i in range(per)]
                    )
                first = (f * rows + r) * cols
                for i in range(per):
                    half = pair[1][i]
                    laid[k, pl.ds(first + i, SUBLANES, stride=per), :] = pair[0][i] * (
                        half + half * jnp.tanh(half)
                    )
                out[first : first + cols, k * LANES : (k + 1) * LANES] = laid[
                    k, first : first + cols
                ].astype(BF16)

    product(0, upa, rawa)
    product(1, upb, rawb)
    conv(0, upa)
    conv(1, upb)


def earlier(totals, peers):
    me = lax.axis_index("tm")
    rows = totals.shape[0]

    def swap(array, bit):
        pairs = [(i, i ^ bit) for i in range(peers)]
        return lax.ppermute(array.astype(BF16), "tm", pairs).astype(F32)

    def joined(mine, other, upper):
        both = jnp.stack([jnp.where(upper, other, mine), jnp.where(upper, mine, other)])
        return both.reshape((-1,) + mine.shape[1:])

    odd, second = lax.rem(me, 2) == 1, lax.rem(me // 2, 2) == 1
    near = swap(totals, 1)
    pair = (totals + near).reshape(2, rows // 2, -1)
    pair = jnp.where(odd, pair[1], pair[0])
    next_pair = swap(pair, 2)
    four = (pair + next_pair).reshape(2, rows // 4, -1)
    running = jnp.where(second, four[1], four[0])
    prior = jnp.zeros_like(running)
    step = 4
    while step < peers:
        got = lax.ppermute(
            running.astype(BF16), "tm", [(i, i + step) for i in range(peers - step)]
        ).astype(F32)
        prior, running = prior + got, running + got
        step *= 2
    prior = joined(prior, swap(prior, 2), second)
    prior = prior + jnp.where(second, next_pair, 0.0)
    prior = joined(prior, swap(prior, 1), odd)
    return prior + jnp.where(odd, near, 0.0)


def local(
    stream,
    queries,
    keys,
    values,
    state_in,
    keysum_in,
    attn_gate,
    ffn_shift,
    ffn_scale,
    w_up,
    conv_weight,
    conv_bias,
):
    frames, rows, cols, width = stream.shape
    heads, head_size = keysum_in.shape
    tokens = rows * cols
    parts = lax.axis_size("space")
    peers = lax.axis_size("tm")
    each = heads // parts
    half = w_up.shape[1] // 2
    half_pad = up_to(half, 2 * LANES)
    deep = w_up.shape[0]
    deep_pad = up_to(deep, 8)
    depth = peers * deep_pad
    place = lax.axis_index("space").astype(jnp.int32).reshape(1)

    def round_space(array, k):
        return lax.ppermute(array, "space", [(i, (i + k) % parts) for i in range(parts)])

    def interleaved(array):
        both = array.reshape(array.shape[0], 2, half)
        both = jnp.concatenate([both[:, :1], 0.5 * both[:, 1:]], axis=1)
        both = jnp.pad(both, ((0, 0), (0, 0), (0, half_pad - half)))
        both = both.reshape(array.shape[0], 2, half_pad // LANES, LANES)
        return both.transpose(0, 2, 1, 3).reshape(array.shape[0], 2 * half_pad)

    height = 48 if deep_pad % 48 == 0 else deep_pad
    weights = pl.pallas_call(
        functools.partial(pack_kernel, half, deep),
        grid=(deep_pad // height,),
        in_specs=[pl.BlockSpec((height, 2 * half), lambda i: (i, 0))],
        out_specs=pl.BlockSpec((height, 2 * half_pad), lambda i: (i, 0)),
        out_shape=jax.ShapeDtypeStruct((deep_pad, 2 * half_pad), BF16),
        compiler_params=PARAMS,
        name="pack",
    )(w_up)
    weights = lax.all_gather(weights, "tm", axis=0).reshape(depth, 2 * half_pad)
    taps = interleaved(conv_weight.reshape(9, 2 * half))
    bias = interleaved(conv_bias.reshape(1, 2 * half))

    def frame_block(*shape):
        return pl.BlockSpec((1,) + shape, lambda f, _: (f,) + (0,) * len(shape))

    def whole(*shape):
        return pl.BlockSpec(shape, lambda f, _: (0,) * len(shape))

    flat = (frames, tokens, width)
    part_shape = (each, head_size, LANES)
    sums = pl.pallas_call(
        functools.partial(kv_kernel, heads, head_size, parts),
        grid_spec=pltpu.PrefetchScalarGridSpec(
            num_scalar_prefetch=1,
            grid=(frames,),
            in_specs=[frame_block(tokens, width)] * 2,
            out_specs=[frame_block(*part_shape)] * parts,
            scratch_shapes=[pltpu.VMEM((heads, head_size, LANES), BF16)],
        ),
        out_shape=[jax.ShapeDtypeStruct((frames,) + part_shape, BF16)] * parts,
        compiler_params=PARAMS,
        name="frame_sums",
    )(place, keys.reshape(flat), values.reshape(flat))
    mine = sums[0].astype(F32)
    for k in range(1, parts):
        mine = mine + round_space(sums[k], k).astype(F32)
    prior = earlier(jnp.sum(mine, axis=0).reshape(each * head_size, LANES), peers)
    prior = prior.reshape(part_shape)
    states = (prior + jnp.cumsum(mine, axis=0)).astype(BF16)
    gathered = [states] + [round_space(states, k) for k in range(1, parts)]
    start = jnp.concatenate(
        [state_in, jnp.broadcast_to(keysum_in[..., None], (heads, head_size, LANES - head_size))],
        axis=-1,
    )
    halos = 1 if parts == 2 else 2
    mixed, x, *edges = pl.pallas_call(
        functools.partial(attn_kernel, heads, head_size, parts, deep, deep_pad, cols),
        grid_spec=pltpu.PrefetchScalarGridSpec(
            num_scalar_prefetch=1,
            grid=(frames,),
            in_specs=[frame_block(tokens, width)] * 2
            + [whole(heads, head_size, LANES)]
            + [whole(1, width)] * 3
            + [frame_block(*part_shape)] * parts,
            out_specs=[frame_block(tokens, width), frame_block(tokens, depth)]
            + [frame_block(cols, depth)] * halos,
            scratch_shapes=[pltpu.VMEM((tokens, width), F32)],
        ),
        out_shape=[
            jax.ShapeDtypeStruct(flat, BF16),
            jax.ShapeDtypeStruct((frames, tokens, depth), BF16),
        ]
        + [jax.ShapeDtypeStruct((frames, cols, depth), BF16)] * halos,
        compiler_params=PARAMS,
        name="attention",
    )(
        place,
        queries.reshape(flat),
        stream.reshape(flat),
        start,
        attn_gate.reshape(1, width),
        ffn_shift.reshape(1, width),
        ffn_scale.reshape(1, width),
        *gathered,
    )
    if halos == 1:
        around = [round_space(edges[0], 1)]
    else:
        around = [
            lax.ppermute(edges[1], "space", [(i, i + 1) for i in range(parts - 1)]),
            lax.ppermute(edges[0], "space", [(i + 1, i) for i in range(parts - 1)]),
        ]
    own = frames * tokens
    total = own + halos * frames * cols

    joined = jnp.concatenate(
        [x.reshape(own, depth)] + [a.reshape(frames * cols, depth) for a in around]
    )

    def column(rows_in, wide):
        return pl.BlockSpec((rows_in, wide), lambda j, _: (0, j))

    hidden = pl.pallas_call(
        functools.partial(ffn_kernel, frames, rows, cols, halos),
        grid_spec=pltpu.PrefetchScalarGridSpec(
            num_scalar_prefetch=1,
            grid=(half_pad // (2 * LANES),),
            in_specs=[pl.BlockSpec(memory_space=pltpu.VMEM)]
            + [column(depth, 4 * LANES), column(9, 4 * LANES), column(1, 4 * LANES)],
            out_specs=column(own, 2 * LANES),
            scratch_shapes=[pltpu.VMEM((2, total, LANES), F32)] * 4
            + [pltpu.VMEM((2, own, LANES), F32)],
        ),
        out_shape=jax.ShapeDtypeStruct((own, half), BF16),
        compiler_params=PARAMS,
        name="mix_ffn",
    )(
        place,
        joined,
        weights,
        taps,
        bias,
    )
    return mixed.reshape(stream.shape), hidden.reshape(frames, rows, cols, half)


def solution(mesh):
    placed = (
        P("tm", "space", None, None),
        P("tm", "space", None, None),
        P("tm", "space", None, None),
        P("tm", "space", None, None),
        P(),
        P(),
        P(),
        P(),
        P(),
        P("tm", None),
        P(),
        P(),
    )
    return jax.shard_map(
        local,
        mesh=mesh,
        in_specs=placed,
        out_specs=(P("tm", "space", None, None), P("tm", "space", None, None)),
        check_vma=False,
    )
```
